32 devices in a mesh: grp: 4 (over z), mem: 8 (over y, x, core).
Axes of the slice: x: 2, y: 2, z: 4, core: 2. Of those that a mesh axis runs over, the one named last changes fastest.
Arguments:
- child_means: float32 [65536, 64], P(('grp', 'mem')), may hold values from -48 to 48
- child_variances: float32 [65536, 64], P(('grp', 'mem')), may hold values from 0.2 to 2
- virtual_counts: int32 [65536], P(('grp', 'mem')), may hold values from 1 to 4
- assignment: int32 [65536, 1], P(('grp', 'mem')), may hold values from 0 to 511
Outputs:
- parent_means: float32 [512, 64], P('mem')
- parent_variances: float32 [512, 64], P('mem')
- parent_weights: float32 [512], P('mem')
The draws below stay inside these ranges and needn't reach their ends.
All inputs are finite; a program needn't handle non-finite values.
Results may differ from the reference program's by a relative error of at most 0.0003.
Values sent between devices are 32-bit elements; how exact they have to be, the bound alone decides.
A program may use at most 64 MiB of HBM per device.

```python
import math
import jax
import jax.numpy as jnp
from jax import lax

D = 64
P_SIZE = 512
ITERS = 2
CHILDREN = 65536


def draw_child_means(key, part):
    return jnp.clip(jax.random.normal(key, (CHILDREN, D), jnp.float32), -6.0, 6.0)


def touch_ends(drawn, key, low, high):
    longest = drawn.shape.index(max(drawn.shape))
    spots = []
    for shift in (0, 1):
        where = [jax.random.randint(jax.random.fold_in(key, axis), (), 0, length) for axis, length in enumerate(drawn.shape)]
        where[longest] = (where[longest] + shift) % drawn.shape[longest]
        spots.append(tuple(where))
    return drawn.at[spots[0]].set(low).at[spots[1]].set(high)


def level_of(stream_key, dims, cuts, least, high):
    gain, own = 1.0, jax.random.fold_in(stream_key, 6)
    for dim, blocks in cuts:
        draws = jnp.exp(jax.random.uniform(jax.random.fold_in(own, dim), (blocks,), jnp.float32, least / len(cuts), high / len(cuts)))
        gain = gain * jnp.repeat(draws, dims[dim] // blocks).reshape([-1 if axis == dim else 1 for axis in range(len(dims))])
    return gain


def distinct(own_key, rows, amount, top, lift):
    ranking = jax.random.permutation(jax.random.fold_in(own_key, 1), amount)
    favour = ranking
    for power in range(3):
        favour = favour * favour // amount
    favour = favour * lift // amount
    lots = jax.random.randint(jax.random.fold_in(own_key, 2), (rows, amount), 0, 4096) + favour
    fixed_rows = jax.random.permutation(jax.random.fold_in(own_key, 3), rows)[jnp.arange(amount) % rows]
    lots = jnp.where(jnp.arange(rows)[:, None] == fixed_rows[None, :], 1 << 14, lots)
    priority = lots * amount + jnp.arange(amount)
    return lax.top_k(priority.astype(jnp.int32), top)[1].astype(jnp.int32)


def setup_inputs(seed: int = 0) -> dict:
    streams_of = jax.random.split(jax.random.key(seed), 5)
    return {
        "child_means": draw_child_means(jax.random.fold_in(streams_of[4], 71), 0),
        "child_variances": jnp.clip(jnp.exp(math.log(2.0) - 2.3025851 * jax.random.uniform(streams_of[1], (CHILDREN, D), jnp.float32) ** level_of(streams_of[1], (CHILDREN, D), ((0, 32),), -0.2, 0.2)), 0.2, 2.0),
        "virtual_counts": touch_ends(jax.random.randint(streams_of[2], (CHILDREN,), 1, 5), jax.random.fold_in(streams_of[2], 1), 1, 4).astype(jnp.int32),
        "assignment": distinct(streams_of[3], CHILDREN, P_SIZE, 1, 0),
    }


def child_features(means, variances):
    return jnp.concatenate([means, variances + means * means], axis=1)


def accumulate(features, extras, weigh):
    row_count = features.shape[0]
    block = math.gcd(row_count, 1024)
    turns = row_count // block
    pieces = (features.reshape(turns, block, features.shape[1]),) + tuple(
        extra.reshape((turns, block) + extra.shape[1:]) for extra in extras)

    def advance(carry, piece):
        weights = weigh(*piece)
        sums = carry[0] + lax.dot_general(weights, piece[0], (((0,), (0,)), ((), ())),
                                          precision=lax.Precision.HIGHEST,
                                          preferred_element_type=jnp.float32)
        counts = carry[1] + jnp.sum(weights, axis=0)
        return (sums, counts), None

    start_sums = (jnp.zeros((P_SIZE, features.shape[1]), jnp.float32), jnp.zeros((P_SIZE,), jnp.float32))
    return lax.scan(advance, start_sums, pieces)[0]


def maximize(counts, sums, total):
    width = sums.shape[1] // 2
    mass = counts + 1.0
    means = sums[:, :width] / mass[:, None]
    second = (sums[:, width:] + 1.0) / mass[:, None]
    return means, second - means * means, mass / (total + P_SIZE)


def parent_table(means, variances, weights):
    inverse = 1.0 / variances
    table = jnp.concatenate([-2.0 * means * inverse, inverse], axis=1)
    offset = jnp.sum(jnp.log(2.0 * math.pi * variances) + means * means * inverse, axis=1)
    return table, offset, jnp.log(weights)


def soft_weights(block_features, block_virtual, table, offset, log_weight):
    width = block_features.shape[1] // 2
    cross = lax.dot_general(block_features, table, (((1,), (1,)), ((), ())),
                            precision=lax.Precision.HIGHEST, preferred_element_type=jnp.float32)
    ell = (-0.5 / width) * (cross + offset[None, :])
    score = log_weight[None, :] + block_virtual[:, None] * ell
    top = jnp.max(score, axis=1, keepdims=True)
    expd = jnp.exp(score - top)
    resp = expd / jnp.sum(expd, axis=1, keepdims=True)
    return resp * block_virtual[:, None]


def reference(child_means, child_variances, virtual_counts, assignment):
    features = child_features(child_means, child_variances)
    virtual = virtual_counts.astype(jnp.float32)
    total = jnp.sum(virtual)
    labels = jnp.arange(P_SIZE, dtype=jnp.int32)

    def initial_weights(block_features, block_virtual, block_assign):
        return (block_assign[:, 0:1] == labels[None, :]).astype(jnp.float32) * block_virtual[:, None]

    sums, counts = accumulate(features, (virtual, assignment), initial_weights)
    means, variances, weights = maximize(counts, sums, total)
    for iteration in range(ITERS):
        table, offset, log_weight = parent_table(means, variances, weights)

        def weigh(block_features, block_virtual):
            return soft_weights(block_features, block_virtual, table, offset, log_weight)

        sums, counts = accumulate(features, (virtual,), weigh)
        means, variances, weights = maximize(counts, sums, total)
    return means, variances, weights
```

```python
import functools
import math

import jax
import jax.numpy as jnp
from jax import lax
from jax.experimental import pallas as pl
from jax.experimental.pallas import tpu as pltpu
from jax.sharding import PartitionSpec as P

P_SIZE = 512
ITERS = 2
LANES = 128
SUB = 8
CHUNK = 512
F32 = jnp.float32
BF16 = jnp.bfloat16
MESH = pl.DeviceIdType.MESH


def split3(value):
    first = value.astype(BF16)
    rest = value - first.astype(F32)
    second = rest.astype(BF16)
    third = (rest - second.astype(F32)).astype(BF16)
    return first, second, third


def dot(left, right):
    return lax.dot_general(left, right, (((1,), (0,)), ((), ())), preferred_element_type=F32)


def kernel(n_mem, n_grp, means_ref, variances_ref, virtual_ref, assign_ref,
           out_means_ref, out_variances_ref, out_weights_ref,
           wide, tall, acc, cnt, shares, landed, groups, tables, virt,
           rs_send, rs_recv, z_send, z_recv, ag_send, ag_recv):
    mem, grp = lax.axis_index("mem"), lax.axis_index("grp")
    width, children = means_ref.shape
    feats = 2 * width
    rows = P_SIZE // n_mem
    turns = children // CHUNK

    def member(step):
        return lax.rem(mem + step, n_mem)

    def group(step):
        return lax.rem(grp + step, n_grp)

    barrier = pltpu.get_barrier_semaphore()
    for step in range(1, n_mem):
        pl.semaphore_signal(barrier, inc=1, device_id={"mem": member(step)}, device_id_type=MESH)
    for step in range(1, n_grp):
        pl.semaphore_signal(barrier, inc=1, device_id={"grp": group(step)}, device_id_type=MESH)

    virt[...] = virtual_ref[...].astype(F32)
    lane = lax.broadcasted_iota(jnp.int32, (rows, LANES), 1)
    diagonal = lane == lax.broadcasted_iota(jnp.int32, (rows, LANES), 0)
    low = lane < width

    def as_row(column):
        return jnp.sum(jnp.where(diagonal, column, 0.0), axis=0, keepdims=True)

    def as_column(row):
        return jnp.sum(jnp.where(diagonal, row, 0.0), axis=1, keepdims=True)

    def fold(weights):
        total = weights[:, :LANES]
        for at in range(LANES, CHUNK, LANES):
            total = total + weights[:, at:at + LANES]
        return total

    def add(turn, sums, counts):
        if turn == 0:
            acc[...] = sums
            cnt[...] = counts
        else:
            acc[...] += sums
            cnt[...] += counts

    def initial(turn):
        span = slice(turn * CHUNK, (turn + 1) * CHUNK)
        mean = means_ref[:, span]
        feature = jnp.concatenate([mean, variances_ref[:, span] + mean * mean], axis=0)
        one, two, three = split3(feature)
        for at, part in enumerate((one, two, three, one, two, one)):
            wide[at * feats:(at + 1) * feats, span] = part
        one, two, three = split3(feature.T)
        for at, part in enumerate((one, two, three)):
            tall[span, at * feats:(at + 1) * feats] = part
        label = lax.broadcasted_iota(jnp.int32, (P_SIZE, CHUNK), 0)
        weights = jnp.where(label == assign_ref[:, span], virt[:, span], 0.0)
        parts = dot(weights.astype(BF16), tall[span, :])
        sums = parts[:, 2 * feats:] + parts[:, feats:2 * feats] + parts[:, :feats]
        add(turn, sums, fold(weights))

    def soft(turn, table, offset, log_weight):
        span = slice(turn * CHUNK, (turn + 1) * CHUNK)
        virtual = virt[:, span]
        score = log_weight + virtual * (dot(table, wide[:, span]) + offset)
        top = jnp.max(score, axis=0, keepdims=True)
        expd = jnp.exp(score - top)
        weights = expd * (virtual / jnp.sum(expd, axis=0, keepdims=True))
        first = weights.astype(BF16)
        second = (weights - first.astype(F32)).astype(BF16)
        high = dot(first, tall[span, :])
        small = dot(second, tall[span, :2 * feats])
        sums = (high[:, 2 * feats:] + small[:, feats:]) + (high[:, feats:2 * feats] + small[:, :feats])
        add(turn, sums + high[:, :feats], fold(weights))

    def combine(turn, local_total):
        counts = jnp.sum(cnt[...], axis=1, keepdims=True)
        for at in range(n_mem):
            span = slice(at * rows, (at + 1) * rows)
            shares[turn, at, :rows, :] = acc[span, :]
            row = as_row(counts[span, :])
            if local_total is not None:
                row = jnp.where(lane[:1, :] == LANES - 1, local_total, row)
            shares[turn, at, rows:, :] = jnp.broadcast_to(row, (SUB, LANES))
        if turn == 0:
            pl.semaphore_wait(barrier, n_mem + n_grp - 2)
        copies = [pltpu.make_async_remote_copy(
            src_ref=shares.at[turn, member(step)], dst_ref=landed.at[turn, step],
            send_sem=rs_send.at[turn, step], recv_sem=rs_recv.at[turn, step],
            device_id={"mem": member(step)}, device_id_type=MESH) for step in range(1, n_mem)]
        for copy in copies:
            copy.start()
        total = shares[turn, mem]
        for step, copy in enumerate(copies, 1):
            copy.wait_recv()
            total = total + landed[turn, step]
        groups[turn, grp] = total
        crossing = [pltpu.make_async_remote_copy(
            src_ref=groups.at[turn, grp], dst_ref=groups.at[turn, grp],
            send_sem=z_send.at[turn, step], recv_sem=z_recv.at[turn, step],
            device_id={"grp": group(step)}, device_id_type=MESH) for step in range(1, n_grp)]
        for copy in crossing:
            copy.start()
        for copy in crossing:
            copy.wait_recv()
        total = groups[turn, 0]
        for at in range(1, n_grp):
            total = total + groups[turn, at]
        return total, copies + crossing

    def maximize(total):
        mass = as_column(total[rows:rows + 1, :]) + 1.0
        scaled = (total[:rows, :] + jnp.where(low, 0.0, 1.0)) / mass
        turned = pltpu.roll(scaled, width, 1)
        means = jnp.where(low, scaled, turned)
        variances = jnp.where(low, turned, scaled) - means * means
        return mass, means, variances

    def spread(turn, mass, means, variances, everything):
        inverse = 1.0 / variances
        scale = -0.5 / width
        terms = jnp.log(2.0 * math.pi * variances) + means * means * inverse
        offset = scale * jnp.sum(jnp.where(low, terms, 0.0), axis=1, keepdims=True)
        log_weight = jnp.log(mass / (everything + P_SIZE))
        tables[turn, mem, :rows, :] = scale * jnp.where(low, -2.0 * means * inverse, inverse)
        tail = lax.broadcasted_iota(jnp.int32, (SUB, LANES), 0) == 0
        tables[turn, mem, rows:, :] = jnp.where(tail, as_row(offset), as_row(log_weight))
        copies = [pltpu.make_async_remote_copy(
            src_ref=tables.at[turn, mem], dst_ref=tables.at[turn, mem],
            send_sem=ag_send.at[turn, step], recv_sem=ag_recv.at[turn, step],
            device_id={"mem": member(step)}, device_id_type=MESH) for step in range(1, n_mem)]
        for copy in copies:
            copy.start()
        for copy in copies:
            copy.wait_recv()
        return copies

    def gathered(turn):
        table = jnp.concatenate([tables[turn, at, :rows, :] for at in range(n_mem)], axis=0)
        offset = jnp.concatenate([as_column(tables[turn, at, rows:rows + 1, :]) for at in range(n_mem)], axis=0)
        log_weight = jnp.concatenate([as_column(tables[turn, at, rows + 1:rows + 2, :]) for at in range(n_mem)], axis=0)
        one, two, three = split3(table)
        return jnp.concatenate([one, one, one, two, two, three], axis=1), offset, log_weight

    for turn in range(turns):
        initial(turn)
    total, sent = combine(0, jnp.sum(virt[...], axis=1, keepdims=True))
    everything = total[rows:rows + 1, LANES - 1:]
    mass, means, variances = maximize(total)
    for iteration in range(ITERS):
        sent += spread(iteration, mass, means, variances, everything)
        parameters = gathered(iteration)
        for turn in range(turns):
            soft(turn, *parameters)
        total, more = combine(iteration + 1, None)
        sent += more
        mass, means, variances = maximize(total)
    out_means_ref[...] = means[:, :width]
    out_variances_ref[...] = variances[:, :width]
    out_weights_ref[...] = as_row(mass / (everything + P_SIZE))[:, :rows]
    for copy in sent:
        copy.wait_send()


def solution(mesh):
    n_grp, n_mem = mesh.shape["grp"], mesh.shape["mem"]
    rows = P_SIZE // n_mem

    def shards(child_means, child_variances, virtual_counts, assignment):
        children, width = child_means.shape
        feats = 2 * width
        rounds = ITERS + 1
        whole = pl.BlockSpec(memory_space=pltpu.VMEM)
        means, variances, weights = pl.pallas_call(
            functools.partial(kernel, n_mem, n_grp),
            out_shape=(
                jax.ShapeDtypeStruct((rows, width), F32),
                jax.ShapeDtypeStruct((rows, width), F32),
                jax.ShapeDtypeStruct((1, rows), F32),
            ),
            in_specs=[whole] * 4,
            out_specs=(whole,) * 3,
            scratch_shapes=[
                pltpu.VMEM((6 * feats, children), BF16),
                pltpu.VMEM((children, 3 * feats), BF16),
                pltpu.VMEM((P_SIZE, feats), F32),
                pltpu.VMEM((P_SIZE, LANES), F32),
                pltpu.VMEM((rounds, n_mem, rows + SUB, LANES), F32),
                pltpu.VMEM((rounds, n_mem, rows + SUB, LANES), F32),
                pltpu.VMEM((rounds, n_grp, rows + SUB, LANES), F32),
                pltpu.VMEM((ITERS, n_mem, rows + SUB, LANES), F32),
                pltpu.VMEM((1, children), F32),
                pltpu.SemaphoreType.DMA((rounds, n_mem)),
                pltpu.SemaphoreType.DMA((rounds, n_mem)),
                pltpu.SemaphoreType.DMA((rounds, n_grp)),
                pltpu.SemaphoreType.DMA((rounds, n_grp)),
                pltpu.SemaphoreType.DMA((ITERS, n_mem)),
                pltpu.SemaphoreType.DMA((ITERS, n_mem)),
            ],
            compiler_params=pltpu.CompilerParams(collective_id=0, has_side_effects=True),
        )(child_means.T, child_variances.T, virtual_counts.reshape(1, children), assignment.T)
        return means, variances, weights.reshape(rows)

    in_specs = (
        P(("grp", "mem"), None),
        P(("grp", "mem"), None),
        P(("grp", "mem")),
        P(("grp", "mem"), None),
    )
    out_specs = (P("mem", None), P("mem", None), P("mem"))
    return jax.shard_map(shards, mesh=mesh, in_specs=in_specs, out_specs=out_specs, check_vma=False)
```

```python
import functools
import math

import jax
import jax.numpy as jnp
from jax import lax
from jax.experimental import pallas as pl
from jax.experimental.pallas import tpu as pltpu
from jax.sharding import PartitionSpec as P

P_SIZE = 512
ITERS = 2
LANES = 128
SUB = 8
CHUNK = 512
PARTS = 2
LOG2E = 1.0 / math.log(2.0)
F32 = jnp.float32
BF16 = jnp.bfloat16
MESH = pl.DeviceIdType.MESH


def split3(value):
    first = value.astype(BF16)
    rest = value - first.astype(F32)
    second = rest.astype(BF16)
    third = (rest - second.astype(F32)).astype(BF16)
    return first, second, third


def dot(left, right):
    return lax.dot_general(left, right, (((1,), (0,)), ((), ())), preferred_element_type=F32)


def kernel(n_mem, n_grp, means_hbm, variances_hbm, virtual_hbm, assign_hbm, packed_ref,
           means_ref, variances_ref, virtual_ref, assign_ref, in_sem,
           wide, tall, scores, first, second, shares, landed, groups, tables, virt,
           rs_send, rs_recv, z_send, z_recv, ag_send, ag_recv):
    mem, grp = lax.axis_index("mem"), lax.axis_index("grp")
    width, children = means_ref.shape
    feats = 2 * width
    rows = P_SIZE // n_mem
    part = rows // PARTS
    block = P_SIZE // PARTS
    turns = children // CHUNK
    mem_steps = tuple(reversed(range(1, n_mem)))
    grp_steps = sorted(range(1, n_grp), key=lambda at: -min(at, n_grp - at))

    def member(step):
        peer, bit = mem, 1
        while bit < n_mem:
            if step & bit:
                peer = peer + bit * (1 - 2 * lax.rem(mem // bit, 2))
            bit *= 2
        return peer

    def group(step):
        return lax.rem(grp + step, n_grp)

    barrier = pltpu.get_barrier_semaphore()
    for step in range(1, n_mem):
        pl.semaphore_signal(barrier, inc=1, device_id={"mem": member(step)}, device_id_type=MESH)
    for step in range(1, n_grp):
        pl.semaphore_signal(barrier, inc=1, device_id={"grp": group(step)}, device_id_type=MESH)

    loads = [pltpu.make_async_copy(source, target, in_sem.at[at]) for at, (source, target) in enumerate((
        (virtual_hbm, virtual_ref), (assign_hbm, assign_ref), (means_hbm, means_ref), (variances_hbm, variances_ref)))]
    for load in loads:
        load.start()
    for load in loads:
        load.wait()
    virt[...] = virtual_ref[...].astype(F32)
    tall[:, 3 * feats:] = jnp.ones((children, LANES), BF16)
    lane = lax.broadcasted_iota(jnp.int32, (part, LANES), 1)
    line = lax.broadcasted_iota(jnp.int32, (part, LANES), 0)
    low = lane < width

    def as_row(column, piece=0):
        return jnp.sum(jnp.where(lane == line + piece * part, column, 0.0), axis=0, keepdims=True)

    def as_column(row):
        return jnp.sum(jnp.where(lane == line, row, 0.0), axis=1, keepdims=True)

    def remote(source, target, send, recv, device):
        return pltpu.make_async_remote_copy(
            src_ref=source, dst_ref=target, send_sem=send, recv_sem=recv, device_id=device, device_id_type=MESH)

    def initial(turn):
        span = slice(turn * CHUNK, (turn + 1) * CHUNK)
        mean = means_ref[:, span]
        feature = jnp.concatenate([mean, variances_ref[:, span] + mean * mean], axis=0)
        one, two, three = split3(feature)
        for at, value in enumerate((one, two, three, one, two, one)):
            wide[at * feats:(at + 1) * feats, span] = value
        one, two, three = split3(feature.T)
        for at, value in enumerate((three, two, one)):
            tall[span, at * feats:(at + 1) * feats] = value
        place = lax.broadcasted_iota(jnp.int32, (P_SIZE, 1), 0)
        owner = lax.rem(place, block)
        label = (owner // part) * rows + (place // block) * part + lax.rem(owner, part)
        weights = jnp.where(label == assign_ref[:, span], virt[:, span], 0.0)
        first[:, span] = weights.astype(BF16)

    def soft(turn):
        span = slice(turn * CHUNK, (turn + 1) * CHUNK)
        score = scores[:, span]
        expd = jnp.exp2(score - jnp.max(score, axis=0, keepdims=True))
        weights = expd * (virt[:, span] / jnp.sum(expd, axis=0, keepdims=True))
        high = weights.astype(BF16)
        first[:, span] = high
        second[:, span] = (weights - high.astype(F32)).astype(BF16)

    def statistics(turn, piece):
        span = slice(piece * block, (piece + 1) * block)
        high = dot(first[span, :], tall[...])
        sums, main, counts = high[:, :feats] + high[:, feats:2 * feats], high[:, 2 * feats:3 * feats], high[:, 3 * feats:]
        if turn > 0:
            small = dot(second[span, :], tall[:, 2 * feats:])
            sums, counts = sums + small[:, :feats], counts + small[:, feats:]
        return sums + main, counts

    def combine(turn, local_total):
        sent, scattered, crossing = [], [], []
        for piece in range(PARTS):
            sums, counts = statistics(turn, piece)
            for at in range(n_mem):
                span = slice(at * part, (at + 1) * part)
                row = as_row(counts[span, :])
                if local_total is not None:
                    row = jnp.where(lane[:1, :] == LANES - 1, local_total, row)
                shares[turn, piece, at, :part, :] = sums[span, :]
                shares[turn, piece, at, part:part + 1, :] = row
            if turn == 0 and piece == 0:
                pl.semaphore_wait(barrier, n_mem + n_grp - 2)
            span = pl.ds(0, part + 1)
            scattered.append([remote(
                shares.at[turn, piece, member(step), span], landed.at[turn, piece, step, span],
                rs_send.at[turn, piece, step], rs_recv.at[turn, piece, step],
                {"mem": member(step)}) for step in mem_steps])
            for copy in scattered[-1]:
                copy.start()
            sent += scattered[-1]
        for piece in range(PARTS):
            total = shares[turn, piece, mem, :part + 1]
            for step, copy in zip(mem_steps, scattered[piece]):
                copy.wait_recv()
                total = total + landed[turn, piece, step, :part + 1]
            groups[turn, piece, grp, :part + 1] = total
            crossing.append([remote(
                groups.at[turn, piece, grp, span], groups.at[turn, piece, grp, span],
                z_send.at[turn, piece, step], z_recv.at[turn, piece, step],
                {"grp": group(step)}) for step in grp_steps])
            for copy in crossing[-1]:
                copy.start()
            sent += crossing[-1]
        return sent, crossing

    def received(turn, piece, crossing):
        for copy in crossing[piece]:
            copy.wait_recv()
        total = groups[turn, piece, 0, :part + 1]
        for at in range(1, n_grp):
            total = total + groups[turn, piece, at, :part + 1]
        return total

    def maximize(total):
        mass = as_column(total[part:part + 1, :]) + 1.0
        scaled = (total[:part, :] + jnp.where(low, 0.0, 1.0)) / mass
        turned = pltpu.roll(scaled, width, 1)
        means = jnp.where(low, scaled, turned)
        variances = jnp.where(low, turned, scaled) - means * means
        return mass, means, variances

    def spread(turn, piece, mass, means, variances, everything):
        inverse = 1.0 / variances
        scale = -0.5 / width * LOG2E
        terms = jnp.log(2.0 * math.pi * variances) + means * means * inverse
        offset = scale * jnp.sum(jnp.where(low, terms, 0.0), axis=1, keepdims=True)
        log_weight = LOG2E * jnp.log(mass / (everything + P_SIZE))
        tables[turn, piece, mem, :part, :] = scale * jnp.where(low, -2.0 * means * inverse, inverse)
        tables[turn, piece, mem, part:part + 1, :] = as_row(offset)
        tables[turn, piece, mem, part + 1:part + 2, :] = as_row(log_weight)
        span = pl.ds(0, part + 2)
        copies = [remote(
            tables.at[turn, piece, mem, span], tables.at[turn, piece, mem, span],
            ag_send.at[turn, piece, step], ag_recv.at[turn, piece, step],
            {"mem": member(step)}) for step in mem_steps]
        for copy in copies:
            copy.start()
        return copies

    def score(turn, piece):
        held = tables.at[turn, piece]
        table = jnp.concatenate([held[at, :part, :] for at in range(n_mem)], axis=0)
        offset = jnp.concatenate([as_column(held[at, part:part + 1, :]) for at in range(n_mem)], axis=0)
        log_weight = jnp.concatenate([as_column(held[at, part + 1:part + 2, :]) for at in range(n_mem)], axis=0)
        one, two, three = split3(table)
        table = jnp.concatenate([one, one, one, two, two, three], axis=1)
        for turn in range(turns):
            span = slice(turn * CHUNK, (turn + 1) * CHUNK)
            scores[piece * block:(piece + 1) * block, span] = (
                log_weight + virt[:, span] * (dot(table, wide[:, span]) + offset))

    for turn in range(turns):
        initial(turn)
    sent, crossing = combine(0, jnp.sum(virt[...], axis=1, keepdims=True))
    everything = None
    for iteration in range(ITERS):
        gathers = []
        for piece in range(PARTS):
            total = received(iteration, piece, crossing)
            if everything is None:
                everything = total[part:part + 1, LANES - 1:]
            gathers.append(spread(iteration, piece, *maximize(total), everything))
        for piece in range(PARTS):
            for copy in gathers[piece]:
                copy.wait_recv()
            score(iteration, piece)
            sent += gathers[piece]
        for turn in range(turns):
            soft(turn)
        more, crossing = combine(iteration + 1, None)
        sent += more
    shown = jnp.zeros((1, LANES), F32)
    for piece in range(PARTS):
        total = received(ITERS, piece, crossing)
        mass, means, variances = maximize(total)
        packed_ref[piece * part:(piece + 1) * part, :] = jnp.where(low, means, variances)
        shown = shown + as_row(mass / (everything + P_SIZE), piece)
    packed_ref[rows:, :] = jnp.broadcast_to(shown, (SUB, LANES))
    for copy in sent:
        copy.wait_send()


def unpack(packed_ref, means_ref, variances_ref, weights_ref):
    rows, width = means_ref.shape
    packed = packed_ref[:rows, :]
    means_ref[...] = packed[:, :width]
    variances_ref[...] = pltpu.roll(packed, width, 1)[:, :width]
    weights_ref[...] = packed_ref[rows:rows + 1, :rows]


def solution(mesh):
    n_grp, n_mem = mesh.shape["grp"], mesh.shape["mem"]
    rows = P_SIZE // n_mem

    def shards(child_means, child_variances, virtual_counts, assignment):
        children, width = child_means.shape
        feats = 2 * width
        rounds = ITERS + 1
        whole = pl.BlockSpec(memory_space=pltpu.VMEM)
        part = rows // PARTS
        packed = pl.pallas_call(
            functools.partial(kernel, n_mem, n_grp),
            out_shape=jax.ShapeDtypeStruct((rows + SUB, LANES), F32),
            in_specs=[pl.BlockSpec(memory_space=pl.ANY)] * 4,
            out_specs=whole,
            scratch_shapes=[
                pltpu.VMEM((width, children), F32),
                pltpu.VMEM((width, children), F32),
                pltpu.VMEM((1, children), jnp.int32),
                pltpu.VMEM((1, children), jnp.int32),
                pltpu.SemaphoreType.DMA((4,)),
                pltpu.VMEM((6 * feats, children), BF16),
                pltpu.VMEM((children, 3 * feats + LANES), BF16),
                pltpu.VMEM((P_SIZE, children), F32),
                pltpu.VMEM((P_SIZE, children), BF16),
                pltpu.VMEM((P_SIZE, children), BF16),
                pltpu.VMEM((rounds, PARTS, n_mem, part + SUB, LANES), F32),
                pltpu.VMEM((rounds, PARTS, n_mem, part + SUB, LANES), F32),
                pltpu.VMEM((rounds, PARTS, n_grp, part + SUB, LANES), F32),
                pltpu.VMEM((ITERS, PARTS, n_mem, part + SUB, LANES), F32),
                pltpu.VMEM((1, children), F32),
                pltpu.SemaphoreType.DMA((rounds, PARTS, n_mem)),
                pltpu.SemaphoreType.DMA((rounds, PARTS, n_mem)),
                pltpu.SemaphoreType.DMA((rounds, PARTS, n_grp)),
                pltpu.SemaphoreType.DMA((rounds, PARTS, n_grp)),
                pltpu.SemaphoreType.DMA((ITERS, PARTS, n_mem)),
                pltpu.SemaphoreType.DMA((ITERS, PARTS, n_mem)),
            ],
            compiler_params=pltpu.CompilerParams(collective_id=0, has_side_effects=True),
        )(child_means.T, child_variances.T, virtual_counts.reshape(1, children), assignment.T)
        means, variances, weights = pl.pallas_call(
            unpack,
            out_shape=(
                jax.ShapeDtypeStruct((rows, width), F32),
                jax.ShapeDtypeStruct((rows, width), F32),
                jax.ShapeDtypeStruct((1, rows), F32),
            ),
            in_specs=[whole],
            out_specs=(whole,) * 3,
        )(packed)
        return means, variances, weights.reshape(rows)

    in_specs = (
        P(("grp", "mem"), None),
        P(("grp", "mem"), None),
        P(("grp", "mem")),
        P(("grp", "mem"), None),
    )
    out_specs = (P("mem", None), P("mem", None), P("mem"))
    return jax.shard_map(shards, mesh=mesh, in_specs=in_specs, out_specs=out_specs, check_vma=False)
```
